256 devices in a mesh: tm: 16 (over z_lo, x), chan: 16 (over z_hi, y, core).
Axes of the slice: x: 4, y: 4, z: 8 (z_hi: 2, z_lo: 4; z = z_hi * 4 + z_lo), core: 2. Of those that a mesh axis runs over, the one named last changes fastest.
Arguments:
- traces: float32 [4096, 16384], P('tm', 'chan'), may hold values from -6 to 6
- band_edges: int32 [2, 4096], replicated, may hold values from 0 to 8191, as said below
- taps: float32 [255], replicated, may hold values from -0.375 to 0.375
- gain_table: float32 [64], replicated, may hold values from 0.3 to 3
- gain_index: int32 [16384], P('chan'), may hold values from 0 to 63
Outputs:
- filtered: float32 [4096, 16384], P('tm', 'chan')
The draws below stay inside these ranges and needn't reach their ends.
Inputs may be any that keep to these rules, and one draw needn't show every extreme that they name: band_edges[0, f] <= band_edges[1, f] for every f.
All inputs are finite; a program needn't handle non-finite values.
Results may differ from the reference program's by a relative error of at most 0.0001.
Values sent between devices are 32-bit elements; how exact they have to be, the bound alone decides.
No kernel may reach another device: no remote copies, remote signals or barrier semaphores. Data moves between devices by JAX's collectives and lax.ppermute only.
A program may use at most 128 MiB of HBM per device.

```python
import math
import jax
import jax.numpy as jnp
from jax import lax

SAMPLES = 4096
CHANNELS = 16384
TAPS = 255
GROUPS = 64


def draw_band_edges(key, part):
    first, second = jax.random.split(key)
    freq = jnp.arange(SAMPLES, dtype=jnp.int32)
    magnitude = jnp.minimum(freq, SAMPLES - freq)
    jitter = jax.random.randint(first, (SAMPLES,), 0, CHANNELS // 128)
    slope = max(1, CHANNELS // SAMPLES)
    high = jnp.minimum(CHANNELS // 2 - 1, CHANNELS // 256 + slope * magnitude + jitter)
    low = jax.random.randint(second, (SAMPLES,), 0, CHANNELS // 256 + 1)
    return jnp.stack([low, high]).astype(jnp.int32)


def touch_ends(array, key, smallest, top_value):
    place = [jax.random.randint(jax.random.fold_in(key, axis), (), 0, length) for axis, length in enumerate(array.shape)]
    longest = array.shape.index(max(array.shape))
    beside = place[:longest] + [(place[longest] + 1) % array.shape[longest]] + place[longest + 1:]
    return array.at[tuple(place)].set(smallest).at[tuple(beside)].set(top_value)


def steps_of(rng, dims, cuts, smallest, high):
    level = 1.0
    for axis_at, shards_of in cuts:
        steps = jax.random.uniform(jax.random.fold_in(jax.random.fold_in(rng, 6), axis_at), (shards_of,), jnp.float32, smallest / len(cuts), high / len(cuts))
        level = level * jnp.repeat(jnp.exp(steps), dims[axis_at] // shards_of).reshape((-1,) + (1,) * (len(dims) - 1 - axis_at))
    return level


def centred(stream_key, dims, spread, bound, pieces=(), kind=jnp.bfloat16):
    values = jax.random.normal(stream_key, dims, jnp.float32) * spread
    if len(pieces) > 0:
        values = steps_of(stream_key, dims, pieces, -0.22, 0.18) * values
    return jnp.clip(values, min=-bound, max=bound).astype(kind)


def setup_inputs(seed: int = 0) -> dict:
    keys = jax.random.split(jax.random.key(seed), 6)
    return {
        "traces": centred(keys[0], (SAMPLES, CHANNELS), 1.0, 6.0, ((0, 16), (1, 16)), jnp.float32),
        "band_edges": draw_band_edges(jax.random.fold_in(keys[5], 71), 0),
        "taps": centred(keys[2], (TAPS,), TAPS ** -0.5, 0.375, (), jnp.float32),
        "gain_table": jnp.clip(jnp.exp(jax.random.uniform(keys[3], (GROUPS,), jnp.float32, math.log(0.3), math.log(3.0))), 0.3, 3.0),
        "gain_index": touch_ends(jax.random.randint(keys[4], (CHANNELS,), 0, GROUPS), jax.random.fold_in(keys[4], 1), 0, GROUPS - 1).astype(jnp.int32),
    }


def toeplitz_tiles(taps):
    count = taps.shape[0]
    centre = (count - 1) // 2
    before = 256 - centre
    after = 512 - before - count
    widened = jnp.concatenate([jnp.zeros((before,), jnp.float32), taps.astype(jnp.float32), jnp.zeros((after,), jnp.float32)])
    tiles = []
    for shift in range(3):
        start = 128 * shift + 128
        reversed_part = widened[start - 127:start + 128][::-1]
        rolled = jnp.concatenate([reversed_part[127:], jnp.zeros((1,), jnp.float32), reversed_part[:127]])
        tiled = jnp.tile(rolled, 128)[: 128 * 255].reshape(128, 255)
        tiles.append(tiled[:, :128])
    return jnp.stack(tiles)


def reference(traces, band_edges, taps, gain_table, gain_index):
    spectrum = jnp.fft.rfft(traces, axis=1)[:, : CHANNELS // 2]
    spectrum = jnp.fft.fft(spectrum, axis=0)
    wave = jnp.arange(CHANNELS // 2, dtype=jnp.int32)[None, :]
    kept = (wave >= band_edges[0][:, None]) & (wave <= band_edges[1][:, None])
    spectrum = jnp.where(kept, spectrum, jnp.zeros_like(spectrum))
    spectrum = jnp.fft.ifft(spectrum, axis=0)
    spectrum = jnp.concatenate([spectrum, jnp.zeros((SAMPLES, 1), spectrum.dtype)], axis=1)
    fanned = jnp.fft.irfft(spectrum, n=CHANNELS, axis=1).astype(jnp.float32)
    padded = jnp.concatenate([jnp.zeros((128, CHANNELS), jnp.float32), fanned, jnp.zeros((128, CHANNELS), jnp.float32)], axis=0)
    tiles = SAMPLES // 128
    blocks = padded.reshape(tiles + 2, 128, CHANNELS)
    kernels = toeplitz_tiles(taps)
    total = jnp.zeros((tiles, 128, CHANNELS), jnp.float32)
    for shift in range(3):
        total = total + jnp.einsum("ab,jac->jbc", kernels[shift], blocks[shift:shift + tiles], precision=lax.Precision.HIGHEST)
    gains = jnp.take(gain_table, gain_index)
    return total.reshape(SAMPLES, CHANNELS) * gains[None, :]
```

```python
import math

import jax
import jax.numpy as jnp
import numpy as np
from jax import lax
from jax.experimental import pallas as pl
from jax.experimental.pallas import tpu as pltpu
from jax.sharding import PartitionSpec as P

f32 = jnp.float32
bf16 = jnp.bfloat16


def circle(product, period):
    theta = (product % period).astype(np.float64) * (2.0 * math.pi / period)
    return np.cos(theta), np.sin(theta)


def halves(table):
    table = np.asarray(table, np.float64)
    high = table.astype(np.float32).astype(jnp.bfloat16)
    low = (table - high.astype(np.float64)).astype(np.float32).astype(jnp.bfloat16)
    return high, low


def channel_tables():
    n = np.arange(128)
    cos, sin = circle(n[:, None] * n[None, :], 128)
    turn_cos, turn_sin = circle(n[:, None] * n[None, :], 16384)
    first = np.concatenate([cos, -sin], axis=0)
    second = np.zeros((2, 128, 2, 2, 32))
    for h in range(2):
        c, s = cos[:, 32 * h : 32 * h + 32], sin[:, 32 * h : 32 * h + 32]
        second[0, :, h, 0], second[1, :, h, 0] = c, s
        second[0, :, h, 1], second[1, :, h, 1] = -s, c
    second = second.reshape(256, 128)
    return first, second, turn_cos.astype(np.float32), turn_sin.astype(np.float32)


def time_tables():
    n = np.arange(128)
    cos, sin = circle(n[:, None] * n[None, :], 128)
    forward = np.block([[cos, sin], [-sin, cos]])
    f1 = np.arange(1024) // 32
    turn_cos, turn_sin = circle(n[:, None] * f1[None, :], 4096)
    f0 = (np.arange(128) // 32) % 2
    m = np.arange(16)
    early_cos, early_sin = circle(m[:, None] * f0[None, :], 32)
    shift_cos, shift_sin = circle(f1[None, :], 32)
    single = lambda *arrays: [np.asarray(a, np.float32) for a in arrays]
    return forward, single(turn_cos, turn_sin, early_cos, early_sin, shift_cos, shift_sin)


def split(x):
    high = x.astype(bf16)
    return high, (x - high.astype(f32)).astype(bf16)


def mm(a, b):
    return jnp.dot(a, b, preferred_element_type=f32)


def left(table_high, table_low, x):
    high, low = split(x)
    return mm(table_high, high) + (mm(table_high, low) + mm(table_low, high))


def right(x, table_high, table_low):
    high, low = split(x)
    return mm(high, table_high) + (mm(low, table_high) + mm(high, table_low))


def lane_bit(rows, bit):
    lane = lax.broadcasted_iota(jnp.int32, (rows, 128), 1)
    return (lane & bit) != 0


def exchange(a, b, mask, bit):
    rolled_b = pltpu.roll(b, bit, 1)
    rolled_a = pltpu.roll(a, 128 - bit, 1)
    return jnp.where(mask, rolled_b, a), jnp.where(mask, b, rolled_a)


def rotate(re, im, angle_num, angle_den, sign):
    num = (angle_num * 8) / angle_den
    if num == 0:
        return re, im
    if num == 2:
        return (im, -re) if sign < 0 else (-im, re)
    if num == 1 or num == 3:
        root = math.sqrt(0.5)
        if sign < 0:
            a, b = (re + im, im - re) if num == 1 else (im - re, -re - im)
        else:
            a, b = (re - im, im + re) if num == 1 else (-re - im, re - im)
        return a * root, b * root
    c = math.cos(2 * math.pi * angle_num / angle_den)
    s = sign * math.sin(2 * math.pi * angle_num / angle_den)
    return re * c - im * s, im * c + re * s


def small_fft(re, im, sign):
    n = len(re)
    if n == 1:
        return re, im
    er, ei = small_fft(re[0::2], im[0::2], sign)
    odd_r, odd_i = small_fft(re[1::2], im[1::2], sign)
    out_r, out_i = [None] * n, [None] * n
    for k in range(n // 2):
        tr, ti = rotate(odd_r[k], odd_i[k], k, n, sign)
        out_r[k], out_i[k] = er[k] + tr, ei[k] + ti
        out_r[k + n // 2], out_i[k + n // 2] = er[k] - tr, ei[k] - ti
    return out_r, out_i


def channel_forward(x, first_h, first_l, second_h, second_l, cos, sin, out):
    mask = lane_bit(128, 64)
    for rl in range(8):
        blocks = []
        for rh in range(2):
            rows = [x[pl.ds(j * 128 + rh * 64 + rl, 8, stride=8), :] for j in range(16)]
            blocks.append(jnp.concatenate(rows, axis=0))
        y = left(first_h[...], first_l[...], jnp.concatenate(blocks, axis=1))
        turned = []
        for rh in range(2):
            yr = y[:128, 128 * rh : 128 * rh + 128]
            yi = y[128:, 128 * rh : 128 * rh + 128]
            c, s = cos[...], sin[...]
            turned.append(jnp.concatenate([yr * c + yi * s, yi * c - yr * s], axis=1))
        o = right(jnp.concatenate(turned, axis=0), second_h[...], second_l[...])
        low, high = exchange(o[:128], o[128:], mask, 64)
        out[pl.ds(rl, 128, stride=16), :] = low
        out[pl.ds(8 + rl, 128, stride=16), :] = high


def channel_inverse(x, first_h, first_l, second_h, second_l, cos, sin, out):
    mask = lane_bit(128, 64)
    for rl in range(8):
        low = x[pl.ds(rl, 128, stride=16), :]
        high = x[pl.ds(8 + rl, 128, stride=16), :]
        pair = exchange(low, high, mask, 64)
        u = right(jnp.concatenate(pair, axis=0), second_h[...], second_l[...])
        turned = []
        for rh in range(2):
            ur = u[128 * rh : 128 * rh + 128, :128]
            ui = u[128 * rh : 128 * rh + 128, 128:]
            c, s = cos[...], sin[...]
            turned.append(jnp.concatenate([ur * c - ui * s, ui * c + ur * s], axis=0))
        o = left(first_h[...], first_l[...], jnp.concatenate(turned, axis=1))
        for rh in range(2):
            for j in range(16):
                out[pl.ds(j * 128 + rh * 64 + rl, 8, stride=8), :] = o[
                    8 * j : 8 * j + 8, 128 * rh : 128 * rh + 128
                ]


def time_part(
    x, factor, fir, fwd_h, fwd_l, inv_h, inv_l, cos2, sin2, cos1, sin1, cos3, sin3,
    out, work, past, future,
):
    bit32, bit64 = lane_bit(8, 32), lane_bit(8, 64)
    for jl in range(8):
        tiles = [x[th * 64 + jl * 8 : th * 64 + jl * 8 + 8, :] for th in range(32)]
        re, im = [], []
        for m in range(16):
            r, i = exchange(tiles[m] + tiles[m + 16], tiles[m] - tiles[m + 16], bit32, 32)
            if m > 0:
                c, s = cos1[m : m + 1, :], sin1[m : m + 1, :]
                r, i = r * c + i * s, i * c - r * s
            re.append(r)
            im.append(i)
        re, im = small_fft(re, im, -1)
        for part, values in ((0, re), (1, im)):
            for g in range(8):
                for rh, value in enumerate(exchange(values[2 * g], values[2 * g + 1], bit64, 64)):
                    row = part * 128 + jl * 16 + rh * 8
                    work[row : row + 8, g * 128 : g * 128 + 128] = value

    fir_h, fir_l = split(fir[...])
    for step in range(4):
        cols = slice(256 * step, 256 * step + 256)
        c, s = cos2[:, cols], sin2[:, cols]
        re, im = work[:128, cols], work[128:, cols]
        b = jnp.concatenate([re * c + im * s, im * c - re * s], axis=0)
        spectrum = left(fwd_h[...], fwd_l[...], b)
        kept = factor[:, cols]
        spectrum = jnp.concatenate([spectrum[:128] * kept, spectrum[128:] * kept], axis=0)
        z = left(inv_h[...], inv_l[...], spectrum)
        re, im = z[:128], z[128:]
        z = jnp.concatenate([re * c - im * s, im * c + re * s], axis=1)
        v = left(fir_h, fir_l, z)
        same, before, after = v[:128], v[128:256], v[256:]
        total, differ = before + after, after - before
        c, s = cos3[:, cols], sin3[:, cols]
        work[:128, cols] = same[:, :256] + (total[:, :256] * c - differ[:, 256:] * s)
        work[128:, cols] = same[:, 256:] + (total[:, 256:] * c + differ[:, :256] * s)
        br, bi = before[:, :256], before[:, 256:]
        wr, wi = br * c + bi * s, bi * c - br * s
        wrapped = jnp.concatenate([wr[:, :128] + wr[:, 128:], wi[:, :128] + wi[:, 128:]], axis=1)
        ahead = jnp.concatenate(
            [after[:, :128] + after[:, 128:256], after[:, 256:384] + after[:, 384:]], axis=1
        )
        if step == 0:
            past[...] = wrapped
            future[...] = ahead
        else:
            past[...] += wrapped
            future[...] += ahead

    for jl in range(8):
        parts = []
        for part in range(2):
            values = [None] * 16
            row = part * 128 + jl * 16
            for g in range(8):
                cols = slice(g * 128, g * 128 + 128)
                values[2 * g], values[2 * g + 1] = exchange(
                    work[row : row + 8, cols], work[row + 8 : row + 16, cols], bit64, 64
                )
            parts.append(values)
        re, im = small_fft(parts[0], parts[1], 1)
        edges = []
        for ref in (past, future):
            sums = []
            for rh in range(2):
                for part in range(2):
                    row = jl * 16 + rh * 8
                    e = ref[row : row + 8, part * 128 : part * 128 + 128]
                    e = e + pltpu.roll(e, 64, 1)
                    sums.append(e + pltpu.roll(e, 32, 1))
            edges.append(
                jnp.where(
                    bit64,
                    jnp.where(bit32, sums[3], sums[2]),
                    jnp.where(bit32, sums[1], sums[0]),
                )
            )
        for m in range(16):
            r, i = re[m], im[m]
            if m > 0:
                c, s = cos1[m : m + 1, :], sin1[m : m + 1, :]
                r, i = r * c - i * s, i * c + r * s
            even, odd = exchange(r, i, bit32, 32)
            early, late = even + odd, even - odd
            if m == 0:
                early = early - edges[0]
            if m == 15:
                late = late - edges[1]
            out[m * 64 + jl * 8 : m * 64 + jl * 8 + 8, :] = early
            out[(m + 16) * 64 + jl * 8 : (m + 16) * 64 + jl * 8 + 8, :] = late


def call(body, args, scratch=()):
    return pl.pallas_call(
        body,
        out_shape=jax.ShapeDtypeStruct((2048, 128), f32),
        in_specs=[pl.BlockSpec(memory_space=pltpu.VMEM)] * len(args),
        out_specs=pl.BlockSpec(memory_space=pltpu.VMEM),
        scratch_shapes=list(scratch),
        compiler_params=pltpu.CompilerParams(vmem_limit_bytes=40 * 1024 * 1024),
        name=body.__name__,
    )(*args)


def forward_kernel(x):
    first, second, cos, sin = channel_tables()
    return call(channel_forward, (x, *halves(first), *halves(second), cos, sin))


def inverse_kernel(x):
    first, second, cos, sin = channel_tables()
    return call(channel_inverse, (x, *halves(first.T), *halves(second.T), cos, sin))


def time_kernel(x, factor, fir):
    forward, tables = time_tables()
    args = (x, factor, fir, *halves(forward), *halves(forward.T), *tables)
    scratch = (
        pltpu.VMEM((256, 1024), f32),
        pltpu.VMEM((128, 256), f32),
        pltpu.VMEM((128, 256), f32),
    )
    return call(time_part, args, scratch)


def fir_matrix(taps):
    padded = jnp.concatenate([jnp.zeros((1,), f32), taps, jnp.zeros((129,), f32)])
    wide = jnp.tile(padded, 128)[: 128 * 384].reshape(128, 384)
    return jnp.concatenate([wide[:, 128:256], wide[:, :128], wide[:, 256:]], axis=0)


def mask_factor(band_edges, owner, scale):
    spread = np.repeat(np.eye(32, dtype=np.float32), 32, axis=1)
    edges = band_edges.astype(f32).reshape(256, 32)
    edges = jnp.dot(edges, spread, precision=lax.Precision.HIGHEST)
    kl = jnp.arange(1024, dtype=jnp.int32) % 32
    wave = owner // 2 + 128 * (32 * (owner % 2) + kl)
    wave_f = wave.astype(f32)[None, :]
    kept = (wave_f >= edges[:128]) & (wave_f <= edges[128:])
    weight = jnp.where(wave == 0, scale, 2.0 * scale).astype(f32)[None, :]
    return jnp.where(kept, weight, 0.0)


def per_device(traces, band_edges, taps, gain_table, gain_index):
    both = ("tm", "chan")
    owner = lax.axis_index("tm") * 16 + lax.axis_index("chan")
    factor = mask_factor(band_edges, owner, 1.0 / (4096 * 16384))
    fir = fir_matrix(taps)
    matches = gain_index[:, None] == jnp.arange(64, dtype=jnp.int32)[None, :]
    gains = jnp.sum(jnp.where(matches, gain_table[None, :], 0.0), axis=1)

    x = traces.reshape(16, 2, 8, 8, 128).transpose(0, 1, 3, 2, 4).reshape(16, 128, 128)
    x = lax.all_to_all(x, "chan", 0, 0, tiled=True).reshape(2048, 128)
    x = forward_kernel(x).reshape(256, 8, 128)
    x = lax.all_to_all(x, both, 0, 0, tiled=True).reshape(2048, 128)
    x = time_kernel(x, factor, fir).reshape(256, 8, 128)
    x = lax.all_to_all(x, both, 0, 0, tiled=True).reshape(2048, 128)
    x = inverse_kernel(x).reshape(16, 128, 128)
    x = lax.all_to_all(x, "chan", 0, 0, tiled=True)
    x = x.reshape(16, 2, 8, 8, 128).transpose(0, 1, 3, 2, 4).reshape(256, 1024)
    return x * gains[None, :]


def solution(mesh):
    in_specs = (P("tm", "chan"), P(), P(), P(), P("chan"))
    return jax.shard_map(
        per_device, mesh=mesh, in_specs=in_specs, out_specs=P("tm", "chan"), check_vma=False
    )
```

```python
import math

import jax
import jax.numpy as jnp
import numpy as np
from jax import lax
from jax.experimental import pallas as pl
from jax.experimental.pallas import tpu as pltpu
from jax.sharding import PartitionSpec as P

f32 = jnp.float32
bf16 = jnp.bfloat16


def circle(product, period):
    theta = (product % period).astype(np.float64) * (2.0 * math.pi / period)
    return np.cos(theta), np.sin(theta)


def halves(table):
    table = np.asarray(table, np.float64)
    high = table.astype(np.float32).astype(jnp.bfloat16)
    low = (table - high.astype(np.float64)).astype(np.float32).astype(jnp.bfloat16)
    return high, low


def channel_tables():
    n = np.arange(128)
    cos, sin = circle(n[:, None] * n[None, :], 128)
    turn_cos, turn_sin = circle(n[:, None] * n[None, :], 16384)
    first = np.concatenate([cos, -sin], axis=0)
    second = np.zeros((2, 128, 2, 2, 32))
    for h in range(2):
        c, s = cos[:, 32 * h : 32 * h + 32], sin[:, 32 * h : 32 * h + 32]
        second[0, :, h, 0], second[1, :, h, 0] = c, s
        second[0, :, h, 1], second[1, :, h, 1] = -s, c
    second = second.reshape(256, 128)
    return first, second, turn_cos.astype(np.float32), turn_sin.astype(np.float32)


def column_f1():
    col = np.arange(1024)
    lane = col % 128
    return 4 * (col // 128) + 2 * ((lane // 32) % 2) + lane // 64


def time_tables():
    n = np.arange(128)
    cos, sin = circle(n[:, None] * n[None, :], 128)
    forward = np.block([[cos, sin], [-sin, cos]])
    f1 = column_f1()
    turn_cos, turn_sin = circle(n[:, None] * f1[None, :], 4096)
    g0 = (np.arange(128) // 32) % 2
    m = np.arange(8)
    early_cos, early_sin = circle(m[:, None] * g0[None, :], 16)
    shift_cos, shift_sin = circle(f1[None, :], 32)
    single = lambda *arrays: [np.asarray(a, np.float32) for a in arrays]
    return forward, single(turn_cos, turn_sin, early_cos, early_sin, shift_cos, shift_sin)


def split(x):
    high = x.astype(bf16)
    return high, (x - high.astype(f32)).astype(bf16)


def mm(a, b):
    return jnp.dot(a, b, preferred_element_type=f32)


def left_table(table):
    high, low = halves(table)
    return np.concatenate([high, high, low], axis=1)


def right_table(table):
    high, low = halves(table)
    return np.concatenate([high, high, low], axis=0)


def left(table, x):
    high, low = split(x)
    return mm(table, jnp.concatenate([high, low, high], axis=0))


def right(x, table):
    high, low = split(x)
    return mm(jnp.concatenate([high, low, high], axis=1), table)


def lane_bit(rows, bit):
    lane = lax.broadcasted_iota(jnp.int32, (rows, 128), 1)
    return (lane & bit) != 0


def exchange(a, b, mask, bit):
    rolled_b = pltpu.roll(b, bit, 1)
    rolled_a = pltpu.roll(a, 128 - bit, 1)
    return jnp.where(mask, rolled_b, a), jnp.where(mask, b, rolled_a)


def rotate(re, im, angle_num, angle_den, sign):
    num = (angle_num * 8) / angle_den
    if num == 0:
        return re, im
    if num == 2:
        return (im, -re) if sign < 0 else (-im, re)
    if num == 1 or num == 3:
        root = math.sqrt(0.5)
        if sign < 0:
            a, b = (re + im, im - re) if num == 1 else (im - re, -re - im)
        else:
            a, b = (re - im, im + re) if num == 1 else (-re - im, re - im)
        return a * root, b * root
    c = math.cos(2 * math.pi * angle_num / angle_den)
    s = sign * math.sin(2 * math.pi * angle_num / angle_den)
    return re * c - im * s, im * c + re * s


def small_fft(re, im, sign):
    n = len(re)
    if n == 1:
        return re, im
    er, ei = small_fft(re[0::2], im[0::2], sign)
    odd_r, odd_i = small_fft(re[1::2], im[1::2], sign)
    out_r, out_i = [None] * n, [None] * n
    for k in range(n // 2):
        tr, ti = rotate(odd_r[k], odd_i[k], k, n, sign)
        out_r[k], out_i[k] = er[k] + tr, ei[k] + ti
        out_r[k + n // 2], out_i[k + n // 2] = er[k] - tr, ei[k] - ti
    return out_r, out_i


def turned_tables(cos, sin, phase, cos_b, sin_b):
    pc, ps = phase[0:1, :], phase[1:2, :]
    cos_b[...] = cos[...] * pc - sin[...] * ps
    sin_b[...] = sin[...] * pc + cos[...] * ps


def channel_forward(x, first, second, cos, sin, phase, out, cos_b, sin_b):
    turned_tables(cos, sin, phase, cos_b, sin_b)
    mask = lane_bit(128, 64)
    for rl in range(8):
        early = x[pl.ds(rl, 128, stride=8), :]
        late = x[pl.ds(1024 + rl, 128, stride=8), :]
        y = left(first[...], jnp.concatenate([early + late, early - late], axis=1))
        turned = []
        for f0, (c, s) in enumerate(((cos[...], sin[...]), (cos_b[...], sin_b[...]))):
            yr = y[:128, 128 * f0 : 128 * f0 + 128]
            yi = y[128:, 128 * f0 : 128 * f0 + 128]
            turned.append(jnp.concatenate([yr * c + yi * s, yi * c - yr * s], axis=1))
        o = right(jnp.concatenate(turned, axis=0), second[...])
        low, high = exchange(o[:128], o[128:], mask, 64)
        out[pl.ds(rl, 128, stride=16), :] = low
        out[pl.ds(8 + rl, 128, stride=16), :] = high


def channel_inverse(x, first, second, cos, sin, phase, out, cos_b, sin_b):
    turned_tables(cos, sin, phase, cos_b, sin_b)
    mask = lane_bit(128, 64)
    for rl in range(8):
        low = x[pl.ds(rl, 128, stride=16), :]
        high = x[pl.ds(8 + rl, 128, stride=16), :]
        u = right(jnp.concatenate(exchange(low, high, mask, 64), axis=0), second[...])
        turned = []
        for f0, (c, s) in enumerate(((cos[...], sin[...]), (cos_b[...], sin_b[...]))):
            ur = u[128 * f0 : 128 * f0 + 128, :128]
            ui = u[128 * f0 : 128 * f0 + 128, 128:]
            turned.append(jnp.concatenate([ur * c - ui * s, ui * c + ur * s], axis=0))
        o = left(first[...], jnp.concatenate(turned, axis=1))
        out[pl.ds(rl, 128, stride=8), :] = o[:, :128] + o[:, 128:]
        out[pl.ds(1024 + rl, 128, stride=8), :] = o[:, :128] - o[:, 128:]


def tile_row(m, tile):
    return 8 * (128 * (m % 2) + 16 * (m // 2) + tile)


def time_part(
    x, factor, fir, fwd, inv, cos2, sin2, cos1, sin1, cos3, sin3, out, work, past, future
):
    bit32, bit64 = lane_bit(8, 32), lane_bit(8, 64)
    for tile in range(16):
        rows = [tile_row(m, tile) for m in range(16)]
        values = [x[row : row + 8, :] for row in rows]
        re, im = [], []
        for m in range(8):
            r, i = exchange(values[m] + values[m + 8], values[m] - values[m + 8], bit32, 32)
            if m > 0:
                c, s = cos1[m : m + 1, :], sin1[m : m + 1, :]
                r, i = r * c + i * s, i * c - r * s
            re.append(r)
            im.append(i)
        re, im = small_fft(re, im, -1)
        for g in range(8):
            work[tile * 8 : tile * 8 + 8, g * 128 : g * 128 + 128] = re[g]
            work[128 + tile * 8 : 136 + tile * 8, g * 128 : g * 128 + 128] = im[g]

    fir_high, fir_low = split(fir[...])
    fir_table = jnp.concatenate([fir_high, fir_high, fir_low], axis=1)
    for step in range(4):
        cols = slice(256 * step, 256 * step + 256)
        c, s = cos2[:, cols], sin2[:, cols]
        re, im = work[:128, cols], work[128:, cols]
        b = jnp.concatenate([re * c + im * s, im * c - re * s], axis=0)
        spectrum = left(fwd[...], b)
        kept = factor[:, cols]
        spectrum = jnp.concatenate([spectrum[:128] * kept, spectrum[128:] * kept], axis=0)
        z = left(inv[...], spectrum)
        re, im = z[:128], z[128:]
        v = left(fir_table, jnp.concatenate([re * c - im * s, im * c + re * s], axis=1))
        same, before, after = v[:128], v[128:256], v[256:]
        total, differ = before + after, after - before
        c, s = cos3[:, cols], sin3[:, cols]
        work[:128, cols] = same[:, :256] + (total[:, :256] * c - differ[:, 256:] * s)
        work[128:, cols] = same[:, 256:] + (total[:, 256:] * c + differ[:, :256] * s)
        br, bi = before[:, :256], before[:, 256:]
        wr, wi = br * c + bi * s, bi * c - br * s
        wrapped = jnp.concatenate([wr[:, :128] + wr[:, 128:], wi[:, :128] + wi[:, 128:]], axis=1)
        ahead = jnp.concatenate(
            [after[:, :128] + after[:, 128:256], after[:, 256:384] + after[:, 384:]], axis=1
        )
        if step == 0:
            past[...] = wrapped
            future[...] = ahead
        else:
            past[...] += wrapped
            future[...] += ahead

    last_c, last_s = math.cos(2 * math.pi * 15 / 32), math.sin(2 * math.pi * 15 / 32)
    for tile in range(16):
        rows = slice(tile * 8, tile * 8 + 8)
        below = slice(128 + tile * 8, 136 + tile * 8)
        re = [work[rows, g * 128 : g * 128 + 128] for g in range(8)]
        im = [work[below, g * 128 : g * 128 + 128] for g in range(8)]
        re, im = small_fft(re, im, 1)
        sums = []
        for ref in (past, future):
            for part in range(2):
                e = ref[rows, part * 128 : part * 128 + 128] * 0.5
                e = e + pltpu.roll(e, 64, 1)
                sums.append(e + pltpu.roll(e, 32, 1))
        first_edge = jnp.where(bit32, sums[1], sums[0])
        turned_re = sums[2] * last_c + sums[3] * last_s
        turned_im = sums[3] * last_c - sums[2] * last_s
        last_edge = jnp.where(
            bit64, -jnp.where(bit32, turned_im, turned_re), jnp.where(bit32, sums[3], sums[2])
        )
        for m in range(8):
            r, i = re[m], im[m]
            if m > 0:
                c, s = cos1[m : m + 1, :], sin1[m : m + 1, :]
                r, i = r * c - i * s, i * c + r * s
            even, odd = exchange(r, i, bit32, 32)
            low, high = even + odd, even - odd
            if m == 0:
                low = low - first_edge
            if m == 7:
                high = high - last_edge
            row = tile_row(m, tile)
            out[row : row + 8, :] = low
            row = tile_row(m + 8, tile)
            out[row : row + 8, :] = high


def call(body, args, scratch=()):
    return pl.pallas_call(
        body,
        out_shape=jax.ShapeDtypeStruct((2048, 128), f32),
        in_specs=[pl.BlockSpec(memory_space=pltpu.VMEM)] * len(args),
        out_specs=pl.BlockSpec(memory_space=pltpu.VMEM),
        scratch_shapes=list(scratch),
        compiler_params=pltpu.CompilerParams(vmem_limit_bytes=40 * 1024 * 1024),
        name=body.__name__,
    )(*args)


def forward_kernel(x, phase):
    first, second, cos, sin = channel_tables()
    scratch = [pltpu.VMEM((128, 128), f32)] * 2
    return call(
        channel_forward, (x, left_table(first), right_table(second), cos, sin, phase), scratch
    )


def inverse_kernel(x, phase):
    first, second, cos, sin = channel_tables()
    scratch = [pltpu.VMEM((128, 128), f32)] * 2
    return call(
        channel_inverse, (x, left_table(first.T), right_table(second.T), cos, sin, phase), scratch
    )


def time_kernel(x, factor, fir):
    forward, tables = time_tables()
    args = (x, factor, fir, left_table(forward), left_table(forward.T), *tables)
    scratch = (
        pltpu.VMEM((256, 1024), f32),
        pltpu.VMEM((128, 256), f32),
        pltpu.VMEM((128, 256), f32),
    )
    return call(time_part, args, scratch)


def fir_matrix(taps):
    padded = jnp.concatenate([jnp.zeros((1,), f32), taps, jnp.zeros((129,), f32)])
    wide = jnp.tile(padded, 128)[: 128 * 384].reshape(128, 384)
    return jnp.concatenate([wide[:, 128:256], wide[:, :128], wide[:, 256:]], axis=0)


def mask_factor(band_edges, owner, scale):
    spread = (np.arange(32)[:, None] == column_f1()[None, :]).astype(np.float32)
    edges = band_edges.astype(f32).reshape(256, 32)
    edges = jnp.dot(edges, spread, precision=lax.Precision.HIGHEST)
    kl = jnp.arange(1024, dtype=jnp.int32) % 32
    wave = owner // 2 + 128 * (32 * (owner % 2) + kl)
    wave_f = wave.astype(f32)[None, :]
    kept = (wave_f >= edges[:128]) & (wave_f <= edges[128:])
    weight = jnp.where(wave == 0, scale, 2.0 * scale).astype(f32)[None, :]
    return jnp.where(kept, weight, 0.0)


def device_phase():
    tm = lax.axis_index("tm")
    m = 2 * (tm & 7) + (tm >> 3)
    table = np.stack(circle(np.arange(16), 32), axis=1).astype(np.float32)
    table = np.repeat(table[:, :, None], 128, axis=2)
    return lax.dynamic_index_in_dim(jnp.asarray(table), m, 0, keepdims=False)


def per_device(traces, band_edges, taps, gain_table, gain_index):
    both = ("tm", "chan")
    groups = [[16 * (8 * i + t) + c for i in range(2) for c in range(16)] for t in range(8)]
    owner = lax.axis_index("tm") * 16 + lax.axis_index("chan")
    factor = mask_factor(band_edges, owner, 1.0 / (4096 * 16384))
    fir = fir_matrix(taps)
    phase = device_phase()
    matches = gain_index[:, None] == jnp.arange(64, dtype=jnp.int32)[None, :]
    gains = jnp.sum(jnp.where(matches, gain_table[None, :], 0.0), axis=1)

    x = traces.reshape(32, 8, 8, 128).transpose(0, 2, 1, 3).reshape(32, 64, 128)
    x = lax.all_to_all(x, both, 0, 0, tiled=True, axis_index_groups=groups).reshape(2048, 128)
    x = forward_kernel(x, phase).reshape(256, 8, 128)
    x = lax.all_to_all(x, both, 0, 0, tiled=True).reshape(2048, 128)
    x = time_kernel(x, factor, fir).reshape(256, 8, 128)
    x = lax.all_to_all(x, both, 0, 0, tiled=True).reshape(2048, 128)
    x = inverse_kernel(x, phase).reshape(32, 64, 128)
    x = lax.all_to_all(x, both, 0, 0, tiled=True, axis_index_groups=groups)
    x = x.reshape(32, 8, 8, 128).transpose(0, 2, 1, 3).reshape(256, 1024)
    return x * gains[None, :]


def solution(mesh):
    in_specs = (P("tm", "chan"), P(), P(), P(), P("chan"))
    return jax.shard_map(
        per_device, mesh=mesh, in_specs=in_specs, out_specs=P("tm", "chan"), check_vma=False
    )
```

```python
import math

import jax
import jax.numpy as jnp
import numpy as np
from jax import lax
from jax.experimental import pallas as pl
from jax.experimental.pallas import tpu as pltpu
from jax.sharding import PartitionSpec as P

f32 = jnp.float32
bf16 = jnp.bfloat16


def circle(product, period):
    theta = (product % period).astype(np.float64) * (2.0 * math.pi / period)
    return np.cos(theta), np.sin(theta)


def halves(table):
    table = np.asarray(table, np.float64)
    high = table.astype(np.float32).astype(jnp.bfloat16)
    low = (table - high.astype(np.float64)).astype(np.float32).astype(jnp.bfloat16)
    return high, low


def channel_tables():
    n = np.arange(128)
    cos, sin = circle(n[:, None] * n[None, :], 128)
    turn_cos, turn_sin = circle(n[:, None] * n[None, :], 16384)
    first = np.concatenate([cos, -sin], axis=0)
    second = np.zeros((2, 128, 2, 2, 32))
    for h in range(2):
        c, s = cos[:, 32 * h : 32 * h + 32], sin[:, 32 * h : 32 * h + 32]
        second[0, :, h, 0], second[1, :, h, 0] = c, s
        second[0, :, h, 1], second[1, :, h, 1] = -s, c
    second = second.reshape(256, 128)
    return first, second, turn_cos.astype(np.float32), turn_sin.astype(np.float32)


def column_f1():
    col = np.arange(1024)
    lane = col % 128
    return 4 * (col // 128) + 2 * ((lane // 32) % 2) + lane // 64


def time_tables():
    n = np.arange(128)
    cos, sin = circle(n[:, None] * n[None, :], 128)
    forward = np.block([[cos, sin], [-sin, cos]])
    f1 = column_f1()
    turn_cos, turn_sin = circle(n[:, None] * f1[None, :], 4096)
    g0 = (np.arange(128) // 32) % 2
    m = np.arange(8)
    early_cos, early_sin = circle(m[:, None] * g0[None, :], 16)
    shift_cos, shift_sin = circle(f1[None, :], 32)
    single = lambda *arrays: [np.asarray(a, np.float32) for a in arrays]
    return forward, single(turn_cos, turn_sin, early_cos, early_sin, shift_cos, shift_sin)


def split(x):
    high = x.astype(bf16)
    return high, (x - high.astype(f32)).astype(bf16)


def mm(a, b):
    return jnp.dot(a, b, preferred_element_type=f32)


def left_table(table):
    high, low = halves(table)
    return np.concatenate([high, high, low], axis=1)


def right_table(table):
    high, low = halves(table)
    return np.concatenate([high, high, low], axis=0)


def left(table, x):
    high, low = split(x)
    return mm(table, jnp.concatenate([high, low, high], axis=0))


def left_apart(table, x):
    high, low = split(x)
    k = x.shape[0]
    return mm(table[:, :k], high) + (mm(table[:, :k], low) + mm(table[:, 2 * k :], high))


def left_pair(table, x):
    high, low = split(x)
    k = x.shape[0]
    both = jnp.concatenate([high, low], axis=0)
    return mm(table[:, : 2 * k], both) + mm(table[:, 2 * k :], high)


def right_pair(x, table):
    high, low = split(x)
    k = x.shape[1]
    both = jnp.concatenate([high, low], axis=1)
    return mm(both, table[: 2 * k]) + mm(high, table[2 * k :])


def right(x, table):
    high, low = split(x)
    return mm(jnp.concatenate([high, low, high], axis=1), table)


def lane_bit(rows, bit):
    lane = lax.broadcasted_iota(jnp.int32, (rows, 128), 1)
    return (lane & bit) != 0


def exchange(a, b, mask, bit):
    rolled_b = pltpu.roll(b, bit, 1)
    rolled_a = pltpu.roll(a, 128 - bit, 1)
    return jnp.where(mask, rolled_b, a), jnp.where(mask, b, rolled_a)


def rotate(re, im, angle_num, angle_den, sign):
    num = (angle_num * 8) / angle_den
    if num == 0:
        return re, im
    if num == 2:
        return (im, -re) if sign < 0 else (-im, re)
    if num == 1 or num == 3:
        root = math.sqrt(0.5)
        if sign < 0:
            a, b = (re + im, im - re) if num == 1 else (im - re, -re - im)
        else:
            a, b = (re - im, im + re) if num == 1 else (-re - im, re - im)
        return a * root, b * root
    c = math.cos(2 * math.pi * angle_num / angle_den)
    s = sign * math.sin(2 * math.pi * angle_num / angle_den)
    return re * c - im * s, im * c + re * s


def small_fft(re, im, sign):
    n = len(re)
    if n == 1:
        return re, im
    er, ei = small_fft(re[0::2], im[0::2], sign)
    odd_r, odd_i = small_fft(re[1::2], im[1::2], sign)
    out_r, out_i = [None] * n, [None] * n
    for k in range(n // 2):
        tr, ti = rotate(odd_r[k], odd_i[k], k, n, sign)
        out_r[k], out_i[k] = er[k] + tr, ei[k] + ti
        out_r[k + n // 2], out_i[k + n // 2] = er[k] - tr, ei[k] - ti
    return out_r, out_i


def turned_tables(cos, sin, phase, cos_b, sin_b):
    pc, ps = phase[0:1, :], phase[1:2, :]
    cos_b[...] = cos[...] * pc - sin[...] * ps
    sin_b[...] = sin[...] * pc + cos[...] * ps


def channel_forward(x, first, second, cos, sin, phase, out, cos_b, sin_b):
    turned_tables(cos, sin, phase, cos_b, sin_b)
    mask = lane_bit(128, 64)
    for rl in range(8):
        early = x[pl.ds(rl, 128, stride=8), :]
        late = x[pl.ds(1024 + rl, 128, stride=8), :]
        y = left_apart(first[...], jnp.concatenate([early + late, early - late], axis=1))
        turned = []
        for f0, (c, s) in enumerate(((cos[...], sin[...]), (cos_b[...], sin_b[...]))):
            yr = y[:128, 128 * f0 : 128 * f0 + 128]
            yi = y[128:, 128 * f0 : 128 * f0 + 128]
            turned.append(jnp.concatenate([yr * c + yi * s, yi * c - yr * s], axis=1))
        o = right(jnp.concatenate(turned, axis=0), second[...])
        low, high = exchange(o[:128], o[128:], mask, 64)
        out[pl.ds(rl, 128, stride=16), :] = low
        out[pl.ds(8 + rl, 128, stride=16), :] = high


def channel_inverse(x, first, second, cos, sin, phase, out, cos_b, sin_b):
    turned_tables(cos, sin, phase, cos_b, sin_b)
    mask = lane_bit(128, 64)
    for rl in range(8):
        low = x[pl.ds(rl, 128, stride=16), :]
        high = x[pl.ds(8 + rl, 128, stride=16), :]
        u = right_pair(jnp.concatenate(exchange(low, high, mask, 64), axis=0), second[...])
        turned = []
        for f0, (c, s) in enumerate(((cos[...], sin[...]), (cos_b[...], sin_b[...]))):
            ur = u[128 * f0 : 128 * f0 + 128, :128]
            ui = u[128 * f0 : 128 * f0 + 128, 128:]
            turned.append(jnp.concatenate([ur * c - ui * s, ui * c + ur * s], axis=0))
        o = left_pair(first[...], jnp.concatenate(turned, axis=1))
        out[pl.ds(rl, 128, stride=8), :] = o[:, :128] + o[:, 128:]
        out[pl.ds(1024 + rl, 128, stride=8), :] = o[:, :128] - o[:, 128:]


def tile_row(m, tile):
    return 8 * (128 * (m % 2) + 16 * (m // 2) + tile)


def time_part(
    x, factor, fir, fwd, inv, cos2, sin2, cos1, sin1, cos3, sin3, out, work, past, future
):
    bit32, bit64 = lane_bit(8, 32), lane_bit(8, 64)
    for tile in range(16):
        rows = [tile_row(m, tile) for m in range(16)]
        values = [x[row : row + 8, :] for row in rows]
        re, im = [], []
        for m in range(8):
            r, i = exchange(values[m] + values[m + 8], values[m] - values[m + 8], bit32, 32)
            if m > 0:
                c, s = cos1[m : m + 1, :], sin1[m : m + 1, :]
                r, i = r * c + i * s, i * c - r * s
            re.append(r)
            im.append(i)
        re, im = small_fft(re, im, -1)
        for g in range(8):
            work[tile * 8 : tile * 8 + 8, g * 128 : g * 128 + 128] = re[g]
            work[128 + tile * 8 : 136 + tile * 8, g * 128 : g * 128 + 128] = im[g]

    fir_high, fir_low = split(fir[...])
    fir_table = jnp.concatenate([fir_high, fir_high, fir_low], axis=1)
    for step in range(4):
        cols = slice(256 * step, 256 * step + 256)
        c, s = cos2[:, cols], sin2[:, cols]
        re, im = work[:128, cols], work[128:, cols]
        b = jnp.concatenate([re * c + im * s, im * c - re * s], axis=0)
        spectrum = left(fwd[...], b)
        kept = factor[:, cols]
        spectrum = jnp.concatenate([spectrum[:128] * kept, spectrum[128:] * kept], axis=0)
        z = left(inv[...], spectrum)
        re, im = z[:128], z[128:]
        v = left(fir_table, jnp.concatenate([re * c - im * s, im * c + re * s], axis=1))
        same, before, after = v[:128], v[128:256], v[256:]
        total, differ = before + after, after - before
        c, s = cos3[:, cols], sin3[:, cols]
        work[:128, cols] = same[:, :256] + (total[:, :256] * c - differ[:, 256:] * s)
        work[128:, cols] = same[:, 256:] + (total[:, 256:] * c + differ[:, :256] * s)
        br, bi = before[:, :256], before[:, 256:]
        wr, wi = br * c + bi * s, bi * c - br * s
        wrapped = jnp.concatenate([wr[:, :128] + wr[:, 128:], wi[:, :128] + wi[:, 128:]], axis=1)
        ahead = jnp.concatenate(
            [after[:, :128] + after[:, 128:256], after[:, 256:384] + after[:, 384:]], axis=1
        )
        if step == 0:
            past[...] = wrapped
            future[...] = ahead
        else:
            past[...] += wrapped
            future[...] += ahead

    last_c, last_s = math.cos(2 * math.pi * 15 / 32), math.sin(2 * math.pi * 15 / 32)
    for tile in range(16):
        rows = slice(tile * 8, tile * 8 + 8)
        below = slice(128 + tile * 8, 136 + tile * 8)
        re = [work[rows, g * 128 : g * 128 + 128] for g in range(8)]
        im = [work[below, g * 128 : g * 128 + 128] for g in range(8)]
        re, im = small_fft(re, im, 1)
        sums = []
        for ref in (past, future):
            for part in range(2):
                e = ref[rows, part * 128 : part * 128 + 128] * 0.5
                e = e + pltpu.roll(e, 64, 1)
                sums.append(e + pltpu.roll(e, 32, 1))
        first_edge = jnp.where(bit32, sums[1], sums[0])
        turned_re = sums[2] * last_c + sums[3] * last_s
        turned_im = sums[3] * last_c - sums[2] * last_s
        last_edge = jnp.where(
            bit64, -jnp.where(bit32, turned_im, turned_re), jnp.where(bit32, sums[3], sums[2])
        )
        for m in range(8):
            r, i = re[m], im[m]
            if m > 0:
                c, s = cos1[m : m + 1, :], sin1[m : m + 1, :]
                r, i = r * c - i * s, i * c + r * s
            even, odd = exchange(r, i, bit32, 32)
            low, high = even + odd, even - odd
            if m == 0:
                low = low - first_edge
            if m == 7:
                high = high - last_edge
            row = tile_row(m, tile)
            out[row : row + 8, :] = low
            row = tile_row(m + 8, tile)
            out[row : row + 8, :] = high


def call(body, args, scratch=()):
    return pl.pallas_call(
        body,
        out_shape=jax.ShapeDtypeStruct((2048, 128), f32),
        in_specs=[pl.BlockSpec(memory_space=pltpu.VMEM)] * len(args),
        out_specs=pl.BlockSpec(memory_space=pltpu.VMEM),
        scratch_shapes=list(scratch),
        compiler_params=pltpu.CompilerParams(vmem_limit_bytes=40 * 1024 * 1024),
        name=body.__name__,
    )(*args)


def forward_kernel(x, phase):
    first, second, cos, sin = channel_tables()
    scratch = [pltpu.VMEM((128, 128), f32)] * 2
    return call(
        channel_forward, (x, left_table(first), right_table(second), cos, sin, phase), scratch
    )


def inverse_kernel(x, phase):
    first, second, cos, sin = channel_tables()
    scratch = [pltpu.VMEM((128, 128), f32)] * 2
    return call(
        channel_inverse, (x, left_table(first.T), right_table(second.T), cos, sin, phase), scratch
    )


def time_kernel(x, factor, fir):
    forward, tables = time_tables()
    args = (x, factor, fir, left_table(forward), left_table(forward.T), *tables)
    scratch = (
        pltpu.VMEM((256, 1024), f32),
        pltpu.VMEM((128, 256), f32),
        pltpu.VMEM((128, 256), f32),
    )
    return call(time_part, args, scratch)


def fir_matrix(taps):
    padded = jnp.concatenate([jnp.zeros((1,), f32), taps, jnp.zeros((129,), f32)])
    wide = jnp.tile(padded, 128)[: 128 * 384].reshape(128, 384)
    return jnp.concatenate([wide[:, 128:256], wide[:, :128], wide[:, 256:]], axis=0)


def mask_factor(band_edges, owner, scale):
    spread = (np.arange(32)[:, None] == column_f1()[None, :]).astype(np.float32)
    edges = band_edges.astype(f32).reshape(256, 32)
    edges = jnp.dot(edges, spread, precision=lax.Precision.HIGHEST)
    kl = jnp.arange(1024, dtype=jnp.int32) % 32
    wave = owner // 2 + 128 * (32 * (owner % 2) + kl)
    wave_f = wave.astype(f32)[None, :]
    kept = (wave_f >= edges[:128]) & (wave_f <= edges[128:])
    weight = jnp.where(wave == 0, scale, 2.0 * scale).astype(f32)[None, :]
    return jnp.where(kept, weight, 0.0)


def device_phase():
    tm = lax.axis_index("tm")
    m = 2 * (tm & 7) + (tm >> 3)
    table = np.stack(circle(np.arange(16), 32), axis=1).astype(np.float32)
    table = np.repeat(table[:, :, None], 128, axis=2)
    return lax.dynamic_index_in_dim(jnp.asarray(table), m, 0, keepdims=False)


def per_device(traces, band_edges, taps, gain_table, gain_index):
    both = ("tm", "chan")
    groups = [[16 * (8 * i + t) + c for i in range(2) for c in range(16)] for t in range(8)]
    owner = lax.axis_index("tm") * 16 + lax.axis_index("chan")
    factor = mask_factor(band_edges, owner, 1.0 / (4096 * 16384))
    fir = fir_matrix(taps)
    phase = device_phase()
    matches = gain_index[:, None] == jnp.arange(64, dtype=jnp.int32)[None, :]
    gains = jnp.sum(jnp.where(matches, gain_table[None, :], 0.0), axis=1)

    x = traces.reshape(32, 8, 8, 128).transpose(0, 2, 1, 3).reshape(32, 64, 128)
    x = lax.all_to_all(x, both, 0, 0, tiled=True, axis_index_groups=groups).reshape(2048, 128)
    x, factor, fir, phase, gains = lax.optimization_barrier((x, factor, fir, phase, gains))
    x = forward_kernel(x, phase).reshape(256, 8, 128)
    x = lax.all_to_all(x, both, 0, 0, tiled=True).reshape(2048, 128)
    x = time_kernel(x, factor, fir).reshape(256, 8, 128)
    x = lax.all_to_all(x, both, 0, 0, tiled=True).reshape(2048, 128)
    x = inverse_kernel(x, phase).reshape(32, 64, 128)
    x = lax.all_to_all(x, both, 0, 0, tiled=True, axis_index_groups=groups)
    x = x.reshape(32, 8, 8, 128).transpose(0, 2, 1, 3).reshape(256, 1024)
    return x * gains[None, :]


def solution(mesh):
    in_specs = (P("tm", "chan"), P(), P(), P(), P("chan"))
    return jax.shard_map(
        per_device, mesh=mesh, in_specs=in_specs, out_specs=P("tm", "chan"), check_vma=False
    )
```

```python
import math

import jax
import jax.numpy as jnp
import numpy as np
from jax import lax
from jax.experimental import pallas as pl
from jax.experimental.pallas import tpu as pltpu
from jax.sharding import PartitionSpec as P

f32 = jnp.float32
bf16 = jnp.bfloat16


def circle(product, period):
    theta = (product % period).astype(np.float64) * (2.0 * math.pi / period)
    return np.cos(theta), np.sin(theta)


def halves(table):
    table = np.asarray(table, np.float64)
    high = table.astype(np.float32).astype(jnp.bfloat16)
    low = (table - high.astype(np.float64)).astype(np.float32).astype(jnp.bfloat16)
    return high, low


def channel_tables():
    n = np.arange(128)
    cos, sin = circle(n[:, None] * n[None, :], 128)
    first = np.concatenate([cos[:64], -sin[:64]], axis=0)
    first[64] = cos[64]
    second = np.zeros((2, 128, 4, 2, 32))
    for h in range(4):
        c, s = cos[:, 32 * h : 32 * h + 32], sin[:, 32 * h : 32 * h + 32]
        second[0, :, h, 0], second[1, :, h, 0] = c, s
        second[0, :, h, 1], second[1, :, h, 1] = -s, c
    second = second.reshape(256, 256)
    turn_cos, turn_sin = circle(np.arange(72)[:, None] * n[None, :], 16384)
    return first, second, turn_cos.astype(np.float32), turn_sin.astype(np.float32)


def column_f1():
    col = np.arange(1024)
    lane = col % 128
    return 4 * (col // 128) + 2 * ((lane // 32) % 2) + lane // 64


def time_tables():
    n = np.arange(128)
    cos, sin = circle(n[:, None] * n[None, :], 128)
    forward = np.block([[cos, sin], [-sin, cos]])
    f1 = column_f1()
    turn_cos, turn_sin = circle(n[:, None] * f1[None, :], 4096)
    g0 = (np.arange(128) // 32) % 2
    m = np.arange(8)
    early_cos, early_sin = circle(m[:, None] * g0[None, :], 16)
    shift_cos, shift_sin = circle(f1[None, :], 32)
    single = lambda *arrays: [np.asarray(a, np.float32) for a in arrays]
    return forward, single(turn_cos, turn_sin, early_cos, early_sin, shift_cos, shift_sin)


def split(x):
    high = x.astype(bf16)
    return high, (x - high.astype(f32)).astype(bf16)


def mm(a, b):
    return jnp.dot(a, b, preferred_element_type=f32)


def left_table(table):
    high, low = halves(table)
    return np.concatenate([high, high, low], axis=1)


def right_table(table):
    high, low = halves(table)
    return np.concatenate([high, high, low], axis=0)


def left(table, x):
    high, low = split(x)
    return mm(table, jnp.concatenate([high, low, high], axis=0))


def left_apart(table, x):
    high, low = split(x)
    k = x.shape[0]
    return mm(table[:, :k], high) + (mm(table[:, :k], low) + mm(table[:, 2 * k :], high))


def left_pair(table, x):
    high, low = split(x)
    k = x.shape[0]
    both = jnp.concatenate([high, low], axis=0)
    return mm(table[:, : 2 * k], both) + mm(table[:, 2 * k :], high)


def right_pair(x, table):
    high, low = split(x)
    k = x.shape[1]
    both = jnp.concatenate([high, low], axis=1)
    return mm(both, table[: 2 * k]) + mm(high, table[2 * k :])


def right(x, table):
    high, low = split(x)
    return mm(jnp.concatenate([high, low, high], axis=1), table)


def lane_bit(rows, bit):
    lane = lax.broadcasted_iota(jnp.int32, (rows, 128), 1)
    return (lane & bit) != 0


def exchange(a, b, mask, bit):
    rolled_b = pltpu.roll(b, bit, 1)
    rolled_a = pltpu.roll(a, 128 - bit, 1)
    return jnp.where(mask, rolled_b, a), jnp.where(mask, b, rolled_a)


def rotate(re, im, angle_num, angle_den, sign):
    num = (angle_num * 8) / angle_den
    if num == 0:
        return re, im
    if num == 2:
        return (im, -re) if sign < 0 else (-im, re)
    if num == 1 or num == 3:
        root = math.sqrt(0.5)
        if sign < 0:
            a, b = (re + im, im - re) if num == 1 else (im - re, -re - im)
        else:
            a, b = (re - im, im + re) if num == 1 else (-re - im, re - im)
        return a * root, b * root
    c = math.cos(2 * math.pi * angle_num / angle_den)
    s = sign * math.sin(2 * math.pi * angle_num / angle_den)
    return re * c - im * s, im * c + re * s


def small_fft(re, im, sign):
    n = len(re)
    if n == 1:
        return re, im
    er, ei = small_fft(re[0::2], im[0::2], sign)
    odd_r, odd_i = small_fft(re[1::2], im[1::2], sign)
    out_r, out_i = [None] * n, [None] * n
    for k in range(n // 2):
        tr, ti = rotate(odd_r[k], odd_i[k], k, n, sign)
        out_r[k], out_i[k] = er[k] + tr, ei[k] + ti
        out_r[k + n // 2], out_i[k + n // 2] = er[k] - tr, ei[k] - ti
    return out_r, out_i


def turned_tables(cos, sin, phase, cos_b, sin_b):
    pc, ps = phase[0:1, :], phase[1:2, :]
    cos_b[...] = cos[...] * pc - sin[...] * ps
    sin_b[...] = sin[...] * pc + cos[...] * ps


def channel_forward(x, first, second, cos, sin, phase, out, cos_b, sin_b, middle):
    turned_tables(cos, sin, phase, cos_b, sin_b)
    mask = lane_bit(64, 64)
    top = lax.broadcasted_iota(jnp.int32, (64, 128), 0) == 0
    tables = ((cos, sin), (cos_b, sin_b))
    for rl in range(8):
        early = x[pl.ds(rl, 128, stride=8), :]
        late = x[pl.ds(1024 + rl, 128, stride=8), :]
        y = left_apart(first[...], jnp.concatenate([early + late, early - late], axis=1))
        turned = []
        for f0, (c, s) in enumerate(tables):
            yr = y[:64, 128 * f0 : 128 * f0 + 128]
            yi = y[64:, 128 * f0 : 128 * f0 + 128]
            middle[8 * f0 + rl : 8 * f0 + rl + 1, :] = yi[:1]
            yi = jnp.where(top, 0.0, yi)
            c, s = c[:64, :], s[:64, :]
            turned.append(jnp.concatenate([yr * c + yi * s, yi * c - yr * s], axis=1))
        o = right(jnp.concatenate(turned, axis=0), second[...])
        for half in range(2):
            cols = slice(128 * half, 128 * half + 128)
            low, high = exchange(o[:64, cols], o[64:, cols], mask, 64)
            out[pl.ds(16 * half + rl, 64, stride=32), :] = low
            out[pl.ds(16 * half + 8 + rl, 64, stride=32), :] = high
    turned = []
    for f0, (c, s) in enumerate(tables):
        y = middle[8 * f0 : 8 * f0 + 8, :]
        turned.append(jnp.concatenate([y * c[64:65, :], -(y * s[64:65, :])], axis=1))
    o = right(jnp.concatenate(turned, axis=0), second[...])
    low, high = exchange(o[:8, :128], o[8:, :128], lane_bit(8, 64), 64)
    out[16:24, :] = low
    out[24:32, :] = high


def channel_inverse(x, first, second, cos, sin, phase, out, cos_b, sin_b, middle):
    turned_tables(cos, sin, phase, cos_b, sin_b)
    mask = lane_bit(64, 64)
    top = lax.broadcasted_iota(jnp.int32, (64, 128), 0) == 0
    tables = ((cos, sin), (cos_b, sin_b))
    pair = jnp.concatenate(exchange(x[16:24, :], x[24:32, :], lane_bit(8, 64), 64), axis=0)
    u = right_pair(jnp.concatenate([pair, jnp.zeros_like(pair)], axis=1), second[...])
    for f0, (c, s) in enumerate(tables):
        rows = slice(8 * f0, 8 * f0 + 8)
        middle[rows, :] = u[rows, :128] * c[64:65, :] - u[rows, 128:] * s[64:65, :]
    for rl in range(8):
        halves_of = []
        for half in range(2):
            low = x[pl.ds(16 * half + rl, 64, stride=32), :]
            high = x[pl.ds(16 * half + 8 + rl, 64, stride=32), :]
            pair = jnp.concatenate(exchange(low, high, mask, 64), axis=0)
            halves_of.append(pair)
        upper = jnp.concatenate(
            [jnp.where(top, 0.0, halves_of[1][:64]), jnp.where(top, 0.0, halves_of[1][64:])], axis=0
        )
        u = right_pair(jnp.concatenate([halves_of[0], upper], axis=1), second[...])
        turned = []
        for f0, (c, s) in enumerate(tables):
            ur = u[64 * f0 : 64 * f0 + 64, :128]
            ui = u[64 * f0 : 64 * f0 + 64, 128:]
            c, s = c[:64, :], s[:64, :]
            row = middle[8 * f0 + rl : 8 * f0 + rl + 1, :]
            im = jnp.where(top, row, ui * c + ur * s)
            turned.append(jnp.concatenate([ur * c - ui * s, im], axis=0))
        o = left_pair(first[...], jnp.concatenate(turned, axis=1))
        out[pl.ds(rl, 128, stride=8), :] = o[:, :128] + o[:, 128:]
        out[pl.ds(1024 + rl, 128, stride=8), :] = o[:, :128] - o[:, 128:]


def tile_row(m, tile):
    return 8 * (128 * (m % 2) + 16 * (m // 2) + tile)


def time_part(
    x, factor, fir, fwd, inv, cos2, sin2, cos1, sin1, cos3, sin3, out, work, past, future
):
    bit32, bit64 = lane_bit(8, 32), lane_bit(8, 64)
    for tile in range(16):
        rows = [tile_row(m, tile) for m in range(16)]
        values = [x[row : row + 8, :] for row in rows]
        re, im = [], []
        for m in range(8):
            r, i = exchange(values[m] + values[m + 8], values[m] - values[m + 8], bit32, 32)
            if m > 0:
                c, s = cos1[m : m + 1, :], sin1[m : m + 1, :]
                r, i = r * c + i * s, i * c - r * s
            re.append(r)
            im.append(i)
        re, im = small_fft(re, im, -1)
        for g in range(8):
            work[tile * 8 : tile * 8 + 8, g * 128 : g * 128 + 128] = re[g]
            work[128 + tile * 8 : 136 + tile * 8, g * 128 : g * 128 + 128] = im[g]

    fir_high, fir_low = split(fir[...])
    fir_table = jnp.concatenate([fir_high, fir_high, fir_low], axis=1)
    for step in range(4):
        cols = slice(256 * step, 256 * step + 256)
        c, s = cos2[:, cols], sin2[:, cols]
        re, im = work[:128, cols], work[128:, cols]
        b = jnp.concatenate([re * c + im * s, im * c - re * s], axis=0)
        spectrum = left(fwd[...], b)
        kept = factor[:, cols]
        spectrum = jnp.concatenate([spectrum[:128] * kept, spectrum[128:] * kept], axis=0)
        z = left(inv[...], spectrum)
        re, im = z[:128], z[128:]
        v = left(fir_table, jnp.concatenate([re * c - im * s, im * c + re * s], axis=1))
        same, before, after = v[:128], v[128:256], v[256:]
        total, differ = before + after, after - before
        c, s = cos3[:, cols], sin3[:, cols]
        work[:128, cols] = same[:, :256] + (total[:, :256] * c - differ[:, 256:] * s)
        work[128:, cols] = same[:, 256:] + (total[:, 256:] * c + differ[:, :256] * s)
        br, bi = before[:, :256], before[:, 256:]
        wr, wi = br * c + bi * s, bi * c - br * s
        wrapped = jnp.concatenate([wr[:, :128] + wr[:, 128:], wi[:, :128] + wi[:, 128:]], axis=1)
        ahead = jnp.concatenate(
            [after[:, :128] + after[:, 128:256], after[:, 256:384] + after[:, 384:]], axis=1
        )
        if step == 0:
            past[...] = wrapped
            future[...] = ahead
        else:
            past[...] += wrapped
            future[...] += ahead

    last_c, last_s = math.cos(2 * math.pi * 15 / 32), math.sin(2 * math.pi * 15 / 32)
    for tile in range(16):
        rows = slice(tile * 8, tile * 8 + 8)
        below = slice(128 + tile * 8, 136 + tile * 8)
        re = [work[rows, g * 128 : g * 128 + 128] for g in range(8)]
        im = [work[below, g * 128 : g * 128 + 128] for g in range(8)]
        re, im = small_fft(re, im, 1)
        sums = []
        for ref in (past, future):
            for part in range(2):
                e = ref[rows, part * 128 : part * 128 + 128] * 0.5
                e = e + pltpu.roll(e, 64, 1)
                sums.append(e + pltpu.roll(e, 32, 1))
        first_edge = jnp.where(bit32, sums[1], sums[0])
        turned_re = sums[2] * last_c + sums[3] * last_s
        turned_im = sums[3] * last_c - sums[2] * last_s
        last_edge = jnp.where(
            bit64, -jnp.where(bit32, turned_im, turned_re), jnp.where(bit32, sums[3], sums[2])
        )
        for m in range(8):
            r, i = re[m], im[m]
            if m > 0:
                c, s = cos1[m : m + 1, :], sin1[m : m + 1, :]
                r, i = r * c - i * s, i * c + r * s
            even, odd = exchange(r, i, bit32, 32)
            low, high = even + odd, even - odd
            if m == 0:
                low = low - first_edge
            if m == 7:
                high = high - last_edge
            row = tile_row(m, tile)
            out[row : row + 8, :] = low
            row = tile_row(m + 8, tile)
            out[row : row + 8, :] = high


def call(body, args, scratch=()):
    return pl.pallas_call(
        body,
        out_shape=jax.ShapeDtypeStruct((2048, 128), f32),
        in_specs=[pl.BlockSpec(memory_space=pltpu.VMEM)] * len(args),
        out_specs=pl.BlockSpec(memory_space=pltpu.VMEM),
        scratch_shapes=list(scratch),
        compiler_params=pltpu.CompilerParams(vmem_limit_bytes=40 * 1024 * 1024),
        name=body.__name__,
    )(*args)


def forward_kernel(x, phase):
    first, second, cos, sin = channel_tables()
    scratch = [pltpu.VMEM((72, 128), f32)] * 2 + [pltpu.VMEM((16, 128), f32)]
    return call(
        channel_forward, (x, left_table(first), right_table(second), cos, sin, phase), scratch
    )


def inverse_kernel(x, phase):
    first, second, cos, sin = channel_tables()
    scratch = [pltpu.VMEM((72, 128), f32)] * 2 + [pltpu.VMEM((16, 128), f32)]
    return call(
        channel_inverse, (x, left_table(first.T), right_table(second.T), cos, sin, phase), scratch
    )


def time_kernel(x, factor, fir):
    forward, tables = time_tables()
    args = (x, factor, fir, left_table(forward), left_table(forward.T), *tables)
    scratch = (
        pltpu.VMEM((256, 1024), f32),
        pltpu.VMEM((128, 256), f32),
        pltpu.VMEM((128, 256), f32),
    )
    return call(time_part, args, scratch)


def fir_matrix(taps):
    padded = jnp.concatenate([jnp.zeros((1,), f32), taps, jnp.zeros((129,), f32)])
    wide = jnp.tile(padded, 128)[: 128 * 384].reshape(128, 384)
    return jnp.concatenate([wide[:, 128:256], wide[:, :128], wide[:, 256:]], axis=0)


def mask_factor(band_edges, owner, scale):
    spread = (np.arange(32)[:, None] == column_f1()[None, :]).astype(np.float32)
    k1, h = owner // 4, owner % 4
    conjugate = (h >= 2) & (k1 > 0)
    mirrored = jnp.roll(band_edges[:, ::-1], 1, axis=1)
    edges = jnp.where(conjugate, mirrored, band_edges).astype(f32).reshape(256, 32)
    edges = jnp.dot(edges, spread, precision=lax.Precision.HIGHEST)
    k2 = 32 * h + jnp.arange(1024, dtype=jnp.int32) % 32
    wave = jnp.where(
        k1 > 0,
        jnp.where(conjugate, 16384 - k1 - 128 * k2, k1 + 128 * k2),
        jnp.where(h >= 2, 64 + 128 * (k2 - 64), 128 * k2),
    )
    wave_f = wave.astype(f32)[None, :]
    kept = (wave_f >= edges[:128]) & (wave_f <= edges[128:])
    weight = jnp.where(wave == 0, scale, 2.0 * scale).astype(f32)[None, :]
    return jnp.where(kept, weight, 0.0)


def device_phase():
    tm = lax.axis_index("tm")
    m = 2 * (tm & 7) + (tm >> 3)
    table = np.stack(circle(np.arange(16), 32), axis=1).astype(np.float32)
    table = np.repeat(table[:, :, None], 128, axis=2)
    return lax.dynamic_index_in_dim(jnp.asarray(table), m, 0, keepdims=False)


def per_device(traces, band_edges, taps, gain_table, gain_index):
    both = ("tm", "chan")
    groups = [[16 * (8 * i + t) + c for i in range(2) for c in range(16)] for t in range(8)]
    owner = lax.axis_index("tm") * 16 + lax.axis_index("chan")
    factor = mask_factor(band_edges, owner, 1.0 / (4096 * 16384))
    fir = fir_matrix(taps)
    phase = device_phase()
    matches = gain_index[:, None] == jnp.arange(64, dtype=jnp.int32)[None, :]
    gains = jnp.sum(jnp.where(matches, gain_table[None, :], 0.0), axis=1)

    x = traces.reshape(32, 8, 8, 128).transpose(0, 2, 1, 3).reshape(32, 64, 128)
    x = lax.all_to_all(x, both, 0, 0, tiled=True, axis_index_groups=groups).reshape(2048, 128)
    x, factor, fir, phase, gains = lax.optimization_barrier((x, factor, fir, phase, gains))
    x = forward_kernel(x, phase).reshape(256, 8, 128)
    x = lax.all_to_all(x, both, 0, 0, tiled=True).reshape(2048, 128)
    x = time_kernel(x, factor, fir).reshape(256, 8, 128)
    x = lax.all_to_all(x, both, 0, 0, tiled=True).reshape(2048, 128)
    x = inverse_kernel(x, phase).reshape(32, 64, 128)
    x = lax.all_to_all(x, both, 0, 0, tiled=True, axis_index_groups=groups)
    x = x.reshape(32, 8, 8, 128).transpose(0, 2, 1, 3).reshape(256, 1024)
    return x * gains[None, :]


def solution(mesh):
    in_specs = (P("tm", "chan"), P(), P(), P(), P("chan"))
    return jax.shard_map(
        per_device, mesh=mesh, in_specs=in_specs, out_specs=P("tm", "chan"), check_vma=False
    )
```
